32 devices in a mesh: grp: 4 (over y, core), shard: 8 (over z, x).
Axes of the slice: x: 2, y: 2, z: 4, core: 2. Of those that a mesh axis runs over, the one named last changes fastest.
Arguments:
- queries: bfloat16 [8192, 256], P(('grp', 'shard')), may hold values from -6 to 6
- positive: int32 [8192], P(('grp', 'shard')), may hold values from 0 to 255
- item_feats: bfloat16 [8192, 128], P(('grp', 'shard')), may hold values from -6 to 6
- frequency: int32 [8192], P(('grp', 'shard')), may hold values from 0 to 1048575
- samples: int32 [32, 8, 128], P(('grp', 'shard')), may hold values from 0 to 255
- counts: int32 [32, 8], P(('grp', 'shard')), may hold values from 1 to 128, as said below
- w_in: bfloat16 [128, 4096], replicated, may hold values from -0.5 to 0.5
- w_out: bfloat16 [4096, 256], replicated, may hold values from -0.09375 to 0.09375
Outputs:
- query_grad: float32 [8192, 256], P(('grp', 'shard'))
- w_in_grad: float32 [128, 4096], P(None, 'shard')
- w_out_grad: float32 [4096, 256], P('shard')
The draws below stay inside these ranges and needn't reach their ends.
Inputs may be any that keep to these rules, and one draw needn't show every extreme that they name: samples[d, s, k] is a row of the item block of device s of d's group; slots k >= counts[d, s] are ignored. `counts`: in every group one device receives 128 live rows from every source. `positive`: a row of the query's own device's item block.
All inputs are finite; a program needn't handle non-finite values.
Results may differ from the reference program's by a relative error of at most 0.019.
Values may be sent and summed in bfloat16 or wider, within the bound.
A program may use at most 64 MiB of HBM per device.

```python
import math
import jax
import jax.numpy as jnp
import numpy as np
from jax import lax

EMB = 256
HIDDEN_SIZE = 4096
FEAT = 128
Q_DEV = 256
ITEM_DEV = 256
SLOTS = 128
QUERIES = 8192
ITEMS = 8192
N_GRP = 4
N_SHARD = 8
DEVICES = 32


def draw_counts(key, part):
    level_cap = jax.random.randint(jax.random.fold_in(key, 11), (DEVICES, 1), SLOTS // 4, SLOTS + 1)
    raw_bits = jax.random.randint(jax.random.fold_in(key, 12), (DEVICES, N_SHARD), 0, 1 << 20)
    row_counts = raw_bits % level_cap + 1
    full_owner = jax.random.randint(jax.random.fold_in(key, 13), (N_GRP,), 0, N_SHARD)
    device_ids = jnp.arange(DEVICES)
    is_full = device_ids % N_SHARD == full_owner[device_ids // N_SHARD]
    return jnp.where(is_full[:, None], SLOTS, row_counts).astype(jnp.int32)


def plant(entries, stream_key, least, largest):
    place = [jax.random.randint(jax.random.fold_in(stream_key, axis), (), 0, length) for axis, length in enumerate(entries.shape)]
    main_axis = entries.shape.index(max(entries.shape))
    next_to = place[:main_axis] + [(place[main_axis] + 1) % entries.shape[main_axis]] + place[main_axis + 1:]
    return entries.at[tuple(place)].set(least).at[tuple(next_to)].set(largest)


def shard_levels(own_key, extent, shards, low, top_value):
    def one(dim, shards_of):
        heights = jax.random.uniform(jax.random.fold_in(jax.random.fold_in(own_key, 6), dim), (shards_of,), jnp.float32, low / len(shards), top_value / len(shards))
        return jnp.repeat(jnp.exp(heights), extent[dim] // shards_of).reshape((-1,) + (1,) * (len(extent) - dim - 1))

    factor_of = one(*shards[0])
    for cut in shards[1:]:
        factor_of = factor_of * one(*cut)
    return factor_of


def cumulative_ranks(number_of, lean):
    weights = [(1 << 20) // math.isqrt(standing ** lean) + 1 for standing in range(1, number_of + 1)]
    deviation = 1 + sum(weights) // (1 << 30)
    return np.cumsum(np.array([max(1, weight // deviation) for weight in weights]))


def ranked_ids(key, shape, number_of, slope):
    grid = cumulative_ranks(number_of, slope)
    pick = jax.random.randint(jax.random.fold_in(key, 1), shape, 0, int(grid[number_of - 1]))
    grade = jnp.searchsorted(jnp.asarray(grid, jnp.int32), pick, side="right")
    return jax.random.permutation(jax.random.fold_in(key, 2), number_of)[grade].astype(jnp.int32)


def ranked_wide(own_key, dims, amount, skew):
    weights = [min(1 << octave, amount + 1 - (1 << octave)) * (1 << 20) // math.isqrt((1 << octave) ** skew) + 1 for octave in range((amount + 1).bit_length()) if 1 << octave <= amount]
    deviation = 1 + sum(weights) // (1 << 30)
    table = np.cumsum(np.array([max(1, weight // deviation) for weight in weights]))
    pick = jax.random.randint(jax.random.fold_in(own_key, 1), dims, 0, int(table[len(weights) - 1]))
    start = jnp.left_shift(1, jnp.searchsorted(jnp.asarray(table, jnp.int32), pick, side="right").astype(jnp.int32))
    rank = start - 1 + jax.random.randint(jax.random.fold_in(own_key, 4), dims, 0, 1 << 30) % jnp.minimum(start, amount + 1 - start)
    return jax.random.permutation(jax.random.fold_in(own_key, 2), amount)[rank].astype(jnp.int32)


def bell_draw(own_key, shape, scale, most, shards=(), held_as=jnp.bfloat16):
    drawn = jax.random.normal(own_key, shape, jnp.float32) * scale
    if len(shards) > 0:
        drawn = shard_levels(own_key, shape, shards, -0.22, 0.18) * drawn
    return jnp.clip(drawn, min=-most, max=most).astype(held_as)


def setup_inputs(seed: int = 0) -> dict:
    key_list = jax.random.split(jax.random.key(seed), 9)
    return {
        "queries": bell_draw(key_list[0], (QUERIES, EMB), 1.0, 6.0, ((0, 32),)),
        "positive": plant(jax.random.randint(key_list[1], (QUERIES,), 0, ITEM_DEV), jax.random.fold_in(key_list[1], 1), 0, ITEM_DEV - 1).astype(jnp.int32),
        "item_feats": bell_draw(key_list[2], (ITEMS, FEAT), 1.0, 6.0, ((0, 32),)),
        "frequency": plant(ranked_wide(key_list[3], (ITEMS,), 1048576, 2), jax.random.fold_in(key_list[3], 3), 0, 1048575).astype(jnp.int32),
        "samples": plant(ranked_ids(key_list[4], (DEVICES, N_SHARD, SLOTS), ITEM_DEV, 2), jax.random.fold_in(key_list[4], 3), 0, ITEM_DEV - 1).astype(jnp.int32),
        "counts": draw_counts(jax.random.fold_in(key_list[8], 71), 0),
        "w_in": bell_draw(key_list[6], (FEAT, HIDDEN_SIZE), FEAT ** -0.5, 0.5),
        "w_out": bell_draw(key_list[7], (HIDDEN_SIZE, EMB), HIDDEN_SIZE ** -0.5, 0.09375),
    }


logit_divisor_factor = 0.05
log_base = 4.0
epsilon = 1e-06
masked_logit = -10000.0

def contract_rows(left, right):
    return lax.dot_general(left, right, (((0,), (0,)), ((), ())), preferred_element_type=jnp.float32)

def item_tower(feats, w_in, w_out, freqs):
    preact = jnp.dot(feats, w_in, preferred_element_type=jnp.float32)
    hidden = jnp.maximum(preact, 0.0).astype(jnp.bfloat16)
    raw_emb = jnp.dot(hidden, w_out, preferred_element_type=jnp.float32)
    radius = jnp.sqrt(lax.optimization_barrier(jnp.sum(raw_emb * raw_emb, -1, keepdims=True)) + epsilon)
    unit_emb = raw_emb / radius
    log_bias = (log_base - jnp.log(freqs.astype(jnp.float32) + 1.0)).astype(jnp.bfloat16)
    return (preact, hidden, radius, unit_emb, log_bias)

def query_side(query_rows, pos_local, own_units, contrast_drawn_item, neg_bias, live_slot):
    query_f = query_rows.astype(jnp.float32)
    query_norm = jnp.sqrt(lax.optimization_barrier(jnp.sum(query_f * query_f, -1, keepdims=True)) + epsilon)
    query_unit = query_f / query_norm
    request_vector_narrow = query_unit.astype(jnp.bfloat16)
    matched_entry_list = jnp.take(own_units, pos_local, axis=0)
    matched_logit_value = lax.optimization_barrier(jnp.sum(request_vector_narrow.astype(jnp.float32) * matched_entry_list.astype(jnp.float32), -1)) / logit_divisor_factor
    whole_offset_vector = jnp.where(live_slot, neg_bias.astype(jnp.float32), masked_logit)
    contrast_logit_value = lax.dot_general(request_vector_narrow, contrast_drawn_item, (((1,), (1,)), ((), ())), preferred_element_type=jnp.float32) / logit_divisor_factor + whole_offset_vector[None, :]
    neg_exp = jnp.exp(contrast_logit_value)
    pos_exp = jnp.exp(matched_logit_value)
    total = pos_exp + lax.optimization_barrier(jnp.sum(neg_exp, -1))
    contrast_probability = neg_exp / total[:, None]
    matched_probability = pos_exp / total
    contrast_derivative = (contrast_probability / logit_divisor_factor).astype(jnp.bfloat16)
    matched_derivative = (matched_probability - 1.0) / logit_divisor_factor
    unit_qgrad = jnp.dot(contrast_derivative, contrast_drawn_item, preferred_element_type=jnp.float32) + matched_derivative[:, None] * matched_entry_list.astype(jnp.float32)
    query_grad = (unit_qgrad - query_unit * lax.optimization_barrier(jnp.sum(query_unit * unit_qgrad, -1, keepdims=True))) / query_norm
    row_grad = contract_rows(contrast_derivative, request_vector_narrow).astype(jnp.bfloat16)
    pos_sum = jax.ops.segment_sum(matched_derivative[:, None] * request_vector_narrow.astype(jnp.float32), pos_local, num_segments=own_units.shape[0])
    return (query_grad, row_grad, pos_sum)

def tower_back(feats, w_out, preact, hidden, radius, unit_emb, item_grad):
    raw_grad = ((item_grad - unit_emb * lax.optimization_barrier(jnp.sum(unit_emb * item_grad, -1, keepdims=True))) / radius).astype(jnp.bfloat16)
    w_out_part = contract_rows(hidden, raw_grad)
    hid_grad = lax.dot_general(raw_grad, w_out, (((1,), (1,)), ((), ())), preferred_element_type=jnp.float32)
    pre_grad = jnp.where(preact > 0.0, hid_grad, 0.0).astype(jnp.bfloat16)
    w_in_part = contract_rows(feats, pre_grad)
    return (w_in_part, w_out_part)

def reference(queries, positive, item_feats, frequency, samples, counts, w_in, w_out):
    group_items = N_SHARD * ITEM_DEV

    def per_group(grp_index):
        item_start = grp_index * group_items
        feats = lax.dynamic_slice_in_dim(item_feats, item_start, group_items, 0)
        freqs = lax.dynamic_slice_in_dim(frequency, item_start, group_items, 0)
        preact, hidden, radius, unit_emb, log_bias = item_tower(feats, w_in, w_out, freqs)
        unit_bf = unit_emb.astype(jnp.bfloat16)

        def per_owner(owner_index):
            device = grp_index * N_SHARD + owner_index
            query_rows = lax.dynamic_slice_in_dim(queries, device * Q_DEV, Q_DEV, 0)
            pos_local = lax.dynamic_slice_in_dim(positive, device * Q_DEV, Q_DEV, 0)
            own_samples = lax.dynamic_index_in_dim(samples, device, 0, keepdims=False)
            own_counts = lax.dynamic_index_in_dim(counts, device, 0, keepdims=False)
            flat_index = (jnp.arange(N_SHARD, dtype=jnp.int32)[:, None] * ITEM_DEV + own_samples).reshape(-1).astype(jnp.int32)
            contrast_drawn_item = jnp.take(unit_bf, flat_index, axis=0)
            neg_bias = jnp.take(log_bias, flat_index, axis=0)
            live_slot = (jnp.arange(SLOTS, dtype=jnp.int32)[None, :] < own_counts[:, None]).reshape(-1)
            own_units = lax.dynamic_slice_in_dim(unit_bf, (owner_index * ITEM_DEV).astype(jnp.int32), ITEM_DEV, 0)
            query_grad, row_grad, pos_sum = query_side(query_rows, pos_local, own_units, contrast_drawn_item, neg_bias, live_slot)
            return (query_grad, row_grad, pos_sum, flat_index)
        query_grads, row_grads, pos_sums, flat_all = lax.map(per_owner, jnp.arange(N_SHARD, dtype=jnp.int32))
        item_grad = jax.ops.segment_sum(row_grads.reshape(-1, EMB).astype(jnp.float32), flat_all.reshape(-1), num_segments=group_items)
        item_grad = item_grad + pos_sums.reshape(-1, EMB)

        def per_device(index):
            start = (index * ITEM_DEV).astype(jnp.int32)

            def piece(array):
                return lax.dynamic_slice_in_dim(array, start, ITEM_DEV, 0)
            w_in_part, w_out_part = tower_back(piece(feats), w_out, piece(preact), piece(hidden), piece(radius), piece(unit_emb), piece(item_grad))
            return (w_in_part.astype(jnp.bfloat16).astype(jnp.float32), w_out_part.astype(jnp.bfloat16).astype(jnp.float32))
        w_in_parts, w_out_parts = lax.map(per_device, jnp.arange(N_SHARD, dtype=jnp.int32))
        return (query_grads.reshape(-1, EMB), lax.optimization_barrier(jnp.sum(w_in_parts, 0)), lax.optimization_barrier(jnp.sum(w_out_parts, 0)))
    query_grads, w_in_sums, w_out_sums = lax.map(per_group, jnp.arange(N_GRP, dtype=jnp.int32))
    return (query_grads.reshape(QUERIES, EMB), lax.optimization_barrier(jnp.sum(w_in_sums, 0)), lax.optimization_barrier(jnp.sum(w_out_sums, 0)))
```

```python
import functools
import math

import jax
import jax.numpy as jnp
from jax import lax
from jax.experimental import pallas as pl
from jax.experimental.pallas import tpu as pltpu
from jax.sharding import PartitionSpec as P

inv_temperature = 1.0 / 0.05
log_base = 4.0
epsilon = 1e-06
masked_logit = -10000.0
MESH = pl.DeviceIdType.MESH
F32 = jnp.float32
BF16 = jnp.bfloat16


def mm(left, right, dims):
    return lax.dot_general(left, right, (dims, ((), ())), preferred_element_type=F32)


NN = ((1,), (0,))
NT = ((1,), (1,))
TN = ((0,), (0,))


def kernel(
    dims,
    q_ref, pos_ref, feats_ref, freq_ref, samp_ref, counts_ref, w_in_ref, w_out_ref,
    qg_ref, wig_ref, wog_ref,
    req, fsend, frecv, ngrad, esc, tot, rsend, rrecv, hid, hidt, acc, uq, part, crecv,
    a1, r1y, b1, r1x, c1, r1z,
    a2, r2x, b2, r2y, c2, r2z,
    fin, gath, tmp,
    req_s, req_r, fwd_s, fwd_r, bwd_s, bwd_r, core_s, core_r,
    y1_s, y1_r, x1_s, x1_r, z1_s, z1_r,
    x2_s, x2_r, y2_s, y2_r, z2_s, z2_r, ag_s, ag_r,
):
    n, ngrp, nx, nz, ny, rows = dims
    width = w_out_ref.shape[1]
    items = feats_ref.shape[0]
    slots = samp_ref.shape[2]
    cb = w_out_ref.shape[0] // n
    g = lax.axis_index("grp")
    me = lax.axis_index("shard")
    core, my_y = lax.rem(g, 2), lax.div(g, 2)
    my_x, my_z = lax.rem(me, nx), lax.div(me, nx)

    def shard_dev(p):
        return {"shard": p}

    def grp_dev(p):
        return {"grp": p}

    def y_dev(p):
        return {"grp": p * 2 + core}

    def x_dev(p):
        return {"shard": my_z * nx + p}

    def z_dev(p):
        return {"shard": p * nx + my_x}

    def remote(src, dst, ssem, rsem, dev):
        return pltpu.make_async_remote_copy(
            src_ref=src, dst_ref=dst, send_sem=ssem, recv_sem=rsem,
            device_id=dev, device_id_type=MESH,
        )

    barrier = pltpu.get_barrier_semaphore()
    for i in range(1, n):
        pl.semaphore_signal(
            barrier, inc=1, device_id=shard_dev(lax.rem(me + i, n)), device_id_type=MESH
        )
    for i in range(1, ngrp):
        pl.semaphore_signal(
            barrier, inc=1, device_id=grp_dev(lax.rem(g + i, ngrp)), device_id_type=MESH
        )
    pl.semaphore_wait(barrier, n - 1 + ngrp - 1)

    def req_copy(p, src):
        return remote(samp_ref.at[p], req.at[src], req_s.at[p], req_r.at[src], shard_dev(p))

    def fwd_copy(p, src):
        return remote(fsend.at[p], frecv.at[src], fwd_s.at[p], fwd_r.at[src], shard_dev(p))

    def bwd_copy(p, src):
        return remote(rsend.at[p], rrecv.at[src], bwd_s.at[p], bwd_r.at[src], shard_dev(p))

    def to(i):
        return lax.rem(me + i, n)

    def frm(i):
        return lax.rem(me + n - i, n)

    @pl.loop(1, n)
    def _(i):
        req_copy(to(i), me).start()

    req[pl.ds(me, 1)] = samp_ref[pl.ds(me, 1)]

    acc[...] = jnp.zeros_like(acc)

    @pl.loop(0, n)
    def _(b):
        cols = pl.ds(pl.multiple_of(b * cb, 128), cb)
        pre = mm(feats_ref[...], w_in_ref[:, cols], NN)
        h = jnp.maximum(pre, 0.0).astype(BF16)
        hid[b] = h
        acc[...] += mm(h, w_out_ref[cols, :], NN)

    raw_emb = acc[...]
    radius = jnp.sqrt(jnp.sum(raw_emb * raw_emb, -1, keepdims=True) + epsilon)
    unit = raw_emb / radius
    unit_bf = unit.astype(BF16)
    bias = (log_base - jnp.log(freq_ref[...].astype(F32) + 1.0)).astype(BF16)
    bias16 = jnp.broadcast_to(bias.astype(F32), (16, items)).astype(BF16)

    item_iota = lax.broadcasted_iota(jnp.int32, (items, slots), 0)

    def onehot(row):
        return (item_iota == row).astype(F32).astype(BF16)

    def gather_rows(buf, slot, src):
        pick = onehot(req[src])
        buf[slot, 0:slots, :] = mm(pick, unit_bf, TN).astype(BF16)
        b16 = mm(bias16, pick, NN).astype(BF16)
        for k in range(width // slots):
            buf[slot, slots : slots + 16, k * slots : (k + 1) * slots] = b16

    @pl.loop(1, n)
    def _(i):
        p = to(i)
        req_copy(p, p).wait_recv()
        gather_rows(fsend, p, p)
        fwd_copy(p, me).start()

    gather_rows(frecv, me, me)

    queries = q_ref[...].astype(F32)
    query_norm = jnp.sqrt(jnp.sum(queries * queries, -1, keepdims=True) + epsilon)
    query_unit = queries / query_norm
    query_bf = query_unit.astype(BF16)
    pos_pick = (
        lax.broadcasted_iota(jnp.int32, (items, q_ref.shape[0]), 0) == pos_ref[...]
    ).astype(F32).astype(BF16)
    pos_rows = mm(pos_pick, unit_bf, TN)
    pos_logit = jnp.sum(query_bf.astype(F32) * pos_rows, -1, keepdims=True) * inv_temperature
    pos_exp = jnp.exp(pos_logit)

    @pl.loop(0, n)
    def _(b):
        hidt[b] = hid[b].T

    slot_iota = lax.broadcasted_iota(jnp.int32, (1, slots), 1)

    def logits(src):
        off = frecv[src, slots : slots + 16, 0:slots].astype(F32)[0:1]
        off = jnp.where(slot_iota < counts_ref[0, src], off, masked_logit)
        z = mm(query_bf, frecv[src, 0:slots, :], NT) * inv_temperature + off
        e = jnp.exp(z)
        esc[src] = e
        return e

    tot[...] = logits(me)

    @pl.loop(1, n)
    def _(i):
        src = frm(i)
        fwd_copy(src, src).wait_recv()
        tot[...] += logits(src)

    total = pos_exp + jnp.sum(tot[...], -1, keepdims=True)
    scale = inv_temperature / total
    pos_grad = (pos_exp / total - 1.0) * inv_temperature

    def row_grads(src):
        d = (esc[src] * scale).astype(BF16)
        ngrad[src] = d
        return mm(d, query_bf, TN).astype(BF16)

    @pl.loop(1, n)
    def _(i):
        p = to(i)
        rsend[p] = row_grads(p)
        bwd_copy(p, me).start()

    rrecv[me] = row_grads(me)

    uq[...] = pos_grad * pos_rows

    @pl.loop(0, n)
    def _(b):
        uq[...] += mm(ngrad[b], frecv[b, 0:slots, :], NN)

    unit_qgrad = uq[...]
    qg_ref[...] = (
        unit_qgrad - query_unit * jnp.sum(query_unit * unit_qgrad, -1, keepdims=True)
    ) / query_norm

    pos_term = pos_grad * query_bf.astype(F32)
    high = pos_term.astype(BF16)
    low = (pos_term - high.astype(F32)).astype(BF16)
    acc[...] = mm(pos_pick, high, NN) + mm(pos_pick, low, NN)

    acc[...] += mm(onehot(req[me]), rrecv[me], NN)

    @pl.loop(1, n)
    def _(i):
        src = frm(i)
        bwd_copy(src, src).wait_recv()
        acc[...] += mm(onehot(req[src]), rrecv[src], NN)

    item_grad = acc[...]
    raw_grad = (
        (item_grad - unit * jnp.sum(unit * item_grad, -1, keepdims=True)) / radius
    ).astype(BF16)
    feats = feats_ref[...]

    def core_copy(b):
        return remote(
            part.at[b, 1 - core], crecv.at[b], core_s.at[b], core_r.at[b], grp_dev(g + 1 - 2 * core)
        )

    @pl.loop(0, n)
    def _(b):
        ht = hidt[b]
        wo = mm(ht, raw_grad, NN)
        hg = mm(w_out_ref[pl.ds(pl.multiple_of(b * cb, cb), cb), :], raw_grad, NT)
        pg = jnp.where(ht.astype(F32) > 0.0, hg, 0.0).astype(BF16)
        wi = mm(pg, feats, NN)
        for c in range(2):
            for y in range(ny):
                for h in range(2):
                    r0 = ((c * ny + y) * 2 + h) * rows
                    part[b, c, y, h, :, 0:width] = wo[r0 : r0 + rows].astype(BF16)
                    part[b, c, y, h, :, width:] = wi[r0 : r0 + rows].astype(BF16)
        core_copy(b).start()

    @pl.loop(0, n)
    def _(b):
        core_copy(b).wait_recv()
        bx, bz = lax.rem(b, nx), lax.div(b, nx)
        for y in range(ny):
            a1[y, bx, bz] = (
                part[b, core, y, 0].astype(F32) + crecv[b, y, 0].astype(F32)
            ).astype(BF16)
            a2[bx, y, bz] = (
                part[b, core, y, 1].astype(F32) + crecv[b, y, 1].astype(F32)
            ).astype(BF16)

    def exchange(count, mine, src, dst, ssem, rsem, dev):
        def copy(p, slot):
            return remote(src.at[p], dst.at[slot], ssem.at[p], rsem.at[slot], dev(p))

        def start():
            for i in range(1, count):
                copy(lax.rem(mine + i, count), mine).start()

        def wait_recv():
            for i in range(1, count):
                p = lax.rem(mine + i, count)
                copy(p, p).wait_recv()

        def wait_send():
            for i in range(1, count):
                copy(lax.rem(mine + i, count), mine).wait_send()

        def total_at(*index):
            value = src[(mine, *index)].astype(F32)
            for i in range(1, count):
                value += dst[(lax.rem(mine + i, count), *index)].astype(F32)
            return value.astype(BF16)

        return start, wait_recv, wait_send, total_at

    ex_y1 = exchange(ny, my_y, a1, r1y, y1_s, y1_r, y_dev)
    ex_x1 = exchange(nx, my_x, b1, r1x, x1_s, x1_r, x_dev)
    ex_z1 = exchange(nz, my_z, c1, r1z, z1_s, z1_r, z_dev)
    ex_x2 = exchange(nx, my_x, a2, r2x, x2_s, x2_r, x_dev)
    ex_y2 = exchange(ny, my_y, b2, r2y, y2_s, y2_r, y_dev)
    ex_z2 = exchange(nz, my_z, c2, r2z, z2_s, z2_r, z_dev)

    ex_y1[0]()
    ex_x2[0]()
    ex_y1[1]()

    @pl.loop(0, nz)
    def _(z):
        for x in range(nx):
            b1[x, z] = ex_y1[3](x, z)

    ex_x1[0]()
    ex_x2[1]()

    @pl.loop(0, nz)
    def _(z):
        for y in range(ny):
            b2[y, z] = ex_x2[3](y, z)

    ex_y2[0]()
    ex_x1[1]()

    @pl.loop(0, nz)
    def _(z):
        c1[z] = ex_x1[3](z)

    ex_z1[0]()
    ex_y2[1]()

    @pl.loop(0, nz)
    def _(z):
        c2[z] = ex_y2[3](z)

    ex_z2[0]()
    ex_z1[1]()
    fin[0] = ex_z1[3]()
    ex_z2[1]()
    fin[1] = ex_z2[3]()

    def ag_copy(p, src):
        return remote(fin, gath.at[src], ag_s.at[p], ag_r.at[src], grp_dev(p))

    for i in range(1, ngrp):
        ag_copy(lax.rem(g + i, ngrp), g).start()
    gath[g] = fin[...]

    @pl.loop(1, n)
    def _(i):
        p = to(i)
        req_copy(p, me).wait_send()
        fwd_copy(p, me).wait_send()
        bwd_copy(p, me).wait_send()

    @pl.loop(0, n)
    def _(b):
        core_copy(b).wait_send()

    for ex in (ex_y1, ex_x1, ex_z1, ex_x2, ex_y2, ex_z2):
        ex[2]()

    for i in range(1, ngrp):
        p = lax.rem(g + i, ngrp)
        ag_copy(p, p).wait_recv()
    for c in range(2):
        for y in range(ny):
            for h in range(2):
                r0 = ((c * ny + y) * 2 + h) * rows
                piece = gath[y * 2 + c, h].astype(F32)
                wog_ref[r0 : r0 + rows, :] = piece[:, 0:width]
                tmp[r0 : r0 + rows, :] = piece[:, width:]
    wig_ref[...] = tmp[...].T
    for i in range(1, ngrp):
        ag_copy(lax.rem(g + i, ngrp), g).wait_send()


def local(n, ngrp, queries, positive, item_feats, frequency, samples, counts, w_in, w_out):
    nx = max(1, math.isqrt(n // 2))
    nz = n // nx
    ny = ngrp // 2
    slots = samples.shape[2]
    items, feat = item_feats.shape
    nq, width = queries.shape
    cb = w_out.shape[0] // n
    rows = cb // (4 * ny)
    lanes = width + feat
    dma = lambda k: pltpu.SemaphoreType.DMA((k,))
    vm = lambda *s: pltpu.VMEM(s, BF16)
    vf = lambda *s: pltpu.VMEM(s, F32)
    vspec = pl.BlockSpec(memory_space=pltpu.VMEM)
    return pl.pallas_call(
        functools.partial(kernel, (n, ngrp, nx, nz, ny, rows)),
        out_shape=(
            jax.ShapeDtypeStruct((nq, width), F32),
            jax.ShapeDtypeStruct((feat, cb), F32),
            jax.ShapeDtypeStruct((cb, width), F32),
        ),
        in_specs=[vspec] * 5 + [pl.BlockSpec(memory_space=pltpu.SMEM)] + [vspec] * 2,
        out_specs=(vspec,) * 3,
        scratch_shapes=[
            pltpu.VMEM((n, 1, slots), jnp.int32),
            vm(n, slots + 16, width), vm(n, slots + 16, width),
            vm(n, nq, slots), vf(n, nq, slots), vf(nq, slots),
            vm(n, slots, width), vm(n, slots, width),
            vm(n, items, cb), vm(n, cb, items),
            vf(items, width), vf(nq, width),
            vm(n, 2, ny, 2, rows, lanes), vm(n, ny, 2, rows, lanes),
            vm(ny, nx, nz, rows, lanes), vm(ny, nx, nz, rows, lanes),
            vm(nx, nz, rows, lanes), vm(nx, nz, rows, lanes),
            vm(nz, rows, lanes), vm(nz, rows, lanes),
            vm(nx, ny, nz, rows, lanes), vm(nx, ny, nz, rows, lanes),
            vm(ny, nz, rows, lanes), vm(ny, nz, rows, lanes),
            vm(nz, rows, lanes), vm(nz, rows, lanes),
            vm(2, rows, lanes), vm(ngrp, 2, rows, lanes), vf(cb, feat),
            dma(n), dma(n), dma(n), dma(n), dma(n), dma(n), dma(n), dma(n),
            dma(ny), dma(ny), dma(nx), dma(nx), dma(nz), dma(nz),
            dma(nx), dma(nx), dma(ny), dma(ny), dma(nz), dma(nz), dma(ngrp), dma(ngrp),
        ],
        compiler_params=pltpu.CompilerParams(
            collective_id=0, has_side_effects=True, vmem_limit_bytes=56 * 1024 * 1024
        ),
    )(
        queries,
        positive.reshape(1, nq),
        item_feats,
        frequency.reshape(1, items),
        samples.reshape(n, 1, slots),
        counts,
        w_in,
        w_out,
    )


def solution(mesh):
    in_specs = (
        P(("grp", "shard"), None),
        P(("grp", "shard")),
        P(("grp", "shard"), None),
        P(("grp", "shard")),
        P(("grp", "shard"), None, None),
        P(("grp", "shard"), None),
        P(),
        P(),
    )
    out_specs = (P(("grp", "shard"), None), P(None, "shard"), P("shard", None))
    body = functools.partial(local, mesh.shape["shard"], mesh.shape["grp"])
    return jax.shard_map(body, mesh=mesh, in_specs=in_specs, out_specs=out_specs, check_vma=False)
```

```python
import functools
import math

import jax
import jax.numpy as jnp
from jax import lax
from jax.experimental import pallas as pl
from jax.experimental.pallas import tpu as pltpu
from jax.sharding import PartitionSpec as P

inv_temperature = 1.0 / 0.05
log_base = 4.0
epsilon = 1e-06
masked_logit = -10000.0
MESH = pl.DeviceIdType.MESH
F32 = jnp.float32
BF16 = jnp.bfloat16


def mm(left, right, dims):
    return lax.dot_general(left, right, (dims, ((), ())), preferred_element_type=F32)


NN = ((1,), (0,))
NT = ((1,), (1,))
TN = ((0,), (0,))


def kernel(
    dims,
    q_ref, pos_ref, feats_ref, freq_ref, samp_ref, counts_ref, w_in_ref, w_out_ref,
    qg_ref, sum_ref,
    req, fall, uall, rall, neg, ngrad, esc, tot, rsend, rrecv, hidt, wt, acc, uq,
    woacc, wiacc, part, crecv, yall, gath,
    req_s, req_r, bwd_s, bwd_r, core_s, core_r, y_s, y_r, ag_s, ag_r, *ag_sems,
):
    n, ngrp, nx, nz, ny = dims
    width = w_out_ref.shape[1]
    items = feats_ref.shape[0]
    slots = samp_ref.shape[2]
    cb = w_out_ref.shape[0] // n
    g = lax.axis_index("grp")
    me = lax.axis_index("shard")
    core, my_y = lax.rem(g, 2), lax.div(g, 2)
    my_x, my_z = lax.rem(me, nx), lax.div(me, nx)

    def shard_dev(p):
        return {"shard": p}

    def grp_dev(p):
        return {"grp": p}

    def remote(src, dst, ssem, rsem, dev):
        return pltpu.make_async_remote_copy(
            src_ref=src, dst_ref=dst, send_sem=ssem, recv_sem=rsem,
            device_id=dev, device_id_type=MESH,
        )

    class Gather:
        def __init__(self, buf, split, sems):
            self.buf, self.sems, self.sent = buf, sems, []
            self.parts = (pl.ds(0, split), pl.ds(split, buf.shape[1] - split))

        def copy(self, h, block, ssem, dev):
            ref = self.buf.at[block, self.parts[h]]
            return remote(ref, ref, ssem, self.sems[0].at[h, block], dev)

        def send(self, cond, h, block, kind, dev, x=0):
            ssem = self.sems[kind].at[(h, x, block) if kind == 3 else (h, block)]
            make = lambda: self.copy(h, block, ssem, dev)
            pl.when(cond)(lambda: make().start())
            self.sent.append((cond, make))

        def right(self, cond, h, block):
            self.send(cond & (my_z + 1 < nz), h, block, 1, shard_dev(lax.min(me + nx, n - 1)))

        def left(self, cond, h, block):
            self.send(cond & (my_z >= 1), h, block, 2, shard_dev(lax.max(me - nx, 0)))

        def across(self, cond, h, block):
            for i in range(1, nx):
                x = lax.rem(my_x + i, nx)
                self.send(cond, h, block, 3, shard_dev(my_z * nx + x), x)

        def wait(self, cond, h, block):
            pl.when(cond)(
                lambda: self.copy(h, block, self.sems[1].at[h, block], shard_dev(me)).wait_recv()
            )

        def start(self):
            yes = my_z >= 0
            self.right(yes, 0, me)
            self.left(yes, 0, me)
            self.across(yes, 1, me)
            self.across(yes, 0, me)
            self.right(yes, 1, me)
            self.left(yes, 1, me)

        def step(self, k):
            yes = my_z >= 0
            lo, hi = my_z - k >= 0, my_z + k < nz
            zl, zh = lax.max(my_z - k, 0), lax.min(my_z + k, nz - 1)
            if k == 1:
                for i in range(1, nx):
                    block = my_z * nx + lax.rem(my_x + i, nx)
                    self.wait(yes, 1, block)
                    self.right(yes, 1, block)
                    self.left(yes, 1, block)
            for cond, z, onward in ((lo, zl, self.right), (hi, zh, self.left)):
                block = z * nx + my_x
                self.wait(cond, 0, block)
                onward(cond, 0, block)
                self.across(cond, 0, block)
            for i in range(nx):
                for cond, z, onward in ((lo, zl, self.right), (hi, zh, self.left)):
                    block = z * nx + lax.rem(my_x + i, nx)
                    self.wait(cond, 1, block)
                    onward(cond, 1, block)

        def finish(self, z):
            for i in range(1, nx):
                self.wait(my_z >= 0, 0, z * nx + lax.rem(my_x + i, nx))

        def drain(self):
            for cond, make in self.sent:
                pl.when(cond)(lambda: make().wait_send())

        def run(self, work):
            for k in range(1, nz):
                self.step(k)
                for cond, z in (
                    (my_z - k >= 0, lax.max(my_z - k, 0)),
                    (my_z + k < nz, lax.min(my_z + k, nz - 1)),
                ):
                    pl.when(cond)(lambda: work(z * nx + my_x))
            for i in range(1, nx):
                x = lax.rem(my_x + i, nx)

                @pl.loop(0, nz)
                def _(k):
                    z = lax.rem(my_z + k, nz)
                    self.wait(my_z >= 0, 0, z * nx + x)
                    work(z * nx + x)

    barrier = pltpu.get_barrier_semaphore()
    for i in range(1, n):
        pl.semaphore_signal(
            barrier, inc=1, device_id=shard_dev(lax.rem(me + i, n)), device_id_type=MESH
        )
    for i in range(1, ngrp):
        pl.semaphore_signal(
            barrier, inc=1, device_id=grp_dev(lax.rem(g + i, ngrp)), device_id_type=MESH
        )
    fall[me] = feats_ref[...]
    pl.semaphore_wait(barrier, n - 1 + ngrp - 1)

    def req_copy(p, src):
        return remote(samp_ref.at[p], req.at[src], req_s.at[p], req_r.at[src], shard_dev(p))

    def bwd_copy(p, src):
        return remote(rsend.at[p], rrecv.at[src], bwd_s.at[p], bwd_r.at[src], shard_dev(p))

    def to(i):
        return lax.rem(me + i, n)

    def frm(i):
        return lax.rem(me + n - i, n)

    ag_f = Gather(fall, items // 2, ag_sems[0:4])
    ag_u = Gather(uall, items // 2 + 16, ag_sems[4:8])
    ag_r_ = Gather(rall, items // 2, ag_sems[8:12])

    ag_f.start()

    @pl.loop(1, n)
    def _(i):
        req_copy(to(i), me).start()

    req[pl.ds(me, 1)] = samp_ref[pl.ds(me, 1)]

    acc[...] = jnp.zeros_like(acc)
    for k in range(nz):
        if k > 0:
            ag_f.step(k)

        @pl.loop(k * nx, (k + 1) * nx)
        def _(b):
            cols = pl.ds(pl.multiple_of(b * cb, 128), cb)
            pre = mm(feats_ref[...], w_in_ref[:, cols], NN)
            h = jnp.maximum(pre, 0.0).astype(BF16)
            acc[...] += mm(h, w_out_ref[cols, :], NN)

    raw_emb = acc[...]
    radius = jnp.sqrt(jnp.sum(raw_emb * raw_emb, -1, keepdims=True) + epsilon)
    unit = raw_emb / radius
    unit_bf = unit.astype(BF16)
    bias = (log_base - jnp.log(freq_ref[...].astype(F32) + 1.0)).astype(BF16)
    uall[me, 0:items, :] = unit_bf
    uall[me, items:, :] = jnp.broadcast_to(bias.astype(F32), (16, items)).astype(BF16)
    ag_u.start()

    queries = q_ref[...].astype(F32)
    query_norm = jnp.sqrt(jnp.sum(queries * queries, -1, keepdims=True) + epsilon)
    query_unit = queries / query_norm
    query_bf = query_unit.astype(BF16)
    pos_pick = (
        lax.broadcasted_iota(jnp.int32, (items, q_ref.shape[0]), 0) == pos_ref[...]
    ).astype(F32).astype(BF16)
    pos_rows = mm(pos_pick, unit_bf, TN)
    pos_logit = jnp.sum(query_bf.astype(F32) * pos_rows, -1, keepdims=True) * inv_temperature
    pos_exp = jnp.exp(pos_logit)

    item_iota = lax.broadcasted_iota(jnp.int32, (items, slots), 0)
    slot_iota = lax.broadcasted_iota(jnp.int32, (1, slots), 1)

    def onehot(row):
        return (item_iota == row).astype(F32).astype(BF16)

    tot[...] = jnp.zeros_like(tot)

    def logits(src):
        pick = onehot(samp_ref[src])
        rows = mm(pick, uall[src, 0:items, :], TN).astype(BF16)
        neg[src] = rows
        off = mm(uall[src, items:, :], pick, NN)[0:1]
        off = jnp.where(slot_iota < counts_ref[0, src], off, masked_logit)
        e = jnp.exp(mm(query_bf, rows, NT) * inv_temperature + off)
        esc[src] = e
        tot[...] += e

    logits(me)
    ag_u.run(logits)

    total = pos_exp + jnp.sum(tot[...], -1, keepdims=True)
    scale = inv_temperature / total
    pos_grad = (pos_exp / total - 1.0) * inv_temperature

    def row_grads(src):
        d = (esc[src] * scale).astype(BF16)
        ngrad[src] = d
        return mm(d, query_bf, TN).astype(BF16)

    @pl.loop(1, n)
    def _(i):
        p = to(i)
        rsend[p] = row_grads(p)
        bwd_copy(p, me).start()

    rrecv[me] = row_grads(me)

    uq[...] = pos_grad * pos_rows

    @pl.loop(0, n)
    def _(b):
        uq[...] += mm(ngrad[b], neg[b], NN)

    unit_qgrad = uq[...]
    qg_ref[...] = (
        unit_qgrad - query_unit * jnp.sum(query_unit * unit_qgrad, -1, keepdims=True)
    ) / query_norm

    for z in range(nz):
        ag_f.finish(z)
    wt[...] = w_in_ref[:, pl.ds(pl.multiple_of(me * cb, 128), cb)].astype(F32).T.astype(BF16)

    @pl.loop(0, n)
    def _(b):
        hidt[b] = jnp.maximum(mm(wt[...], fall[b], NT), 0.0).astype(BF16)

    pos_term = pos_grad * query_bf.astype(F32)
    high = pos_term.astype(BF16)
    low = (pos_term - high.astype(F32)).astype(BF16)
    acc[...] = mm(pos_pick, high, NN) + mm(pos_pick, low, NN)
    acc[...] += mm(onehot(req[me]), rrecv[me], NN)

    @pl.loop(1, n)
    def _(i):
        src = frm(i)
        req_copy(src, src).wait_recv()
        pick = onehot(req[src])
        bwd_copy(src, src).wait_recv()
        acc[...] += mm(pick, rrecv[src], NN)

    item_grad = acc[...]
    rall[me] = (
        (item_grad - unit * jnp.sum(unit * item_grad, -1, keepdims=True)) / radius
    ).astype(BF16)
    ag_r_.start()

    woacc[...] = jnp.zeros_like(woacc)
    wiacc[...] = jnp.zeros_like(wiacc)
    block_rows = pl.ds(pl.multiple_of(me * cb, cb), cb)

    def weights(src):
        raw = rall[src]
        ht = hidt[src]
        hg = mm(w_out_ref[block_rows, :], raw, NT)
        pg = jnp.where(ht.astype(F32) > 0.0, hg, 0.0).astype(BF16)
        woacc[...] += mm(ht, raw, NN)
        wiacc[...] += mm(pg, fall[src], NN)

    weights(me)
    ag_r_.run(weights)

    half = cb // 2
    for c in range(2):
        part[c, :, 0:width] = woacc[c * half : (c + 1) * half].astype(BF16)
        part[c, :, width:] = wiacc[c * half : (c + 1) * half].astype(BF16)
    other = grp_dev(g + 1 - 2 * core)
    core_copy = remote(part.at[1 - core], crecv, core_s.at[0], core_r.at[0], other)
    core_copy.start()
    core_copy.wait_recv()
    yall[my_y] = (part[core].astype(F32) + crecv[...].astype(F32)).astype(BF16)

    def y_copy(p, slot):
        return remote(yall.at[my_y], yall.at[slot], y_s.at[p], y_r.at[slot], grp_dev(p * 2 + core))

    for i in range(1, ny):
        y_copy(lax.rem(my_y + i, ny), my_y).start()

    @pl.loop(1, n)
    def _(i):
        p = to(i)
        req_copy(p, me).wait_send()
        bwd_copy(p, me).wait_send()

    core_copy.wait_send()
    for ag in (ag_f, ag_u, ag_r_):
        ag.drain()

    for i in range(1, ny):
        p = lax.rem(my_y + i, ny)
        y_copy(p, p).wait_recv()
    value = yall[0].astype(F32)
    for y in range(1, ny):
        value += yall[y].astype(F32)
    gath[core] = value.astype(BF16)
    ag_copy = remote(gath.at[core], gath.at[core], ag_s.at[0], ag_r.at[0], other)
    ag_copy.start()
    for i in range(1, ny):
        y_copy(lax.rem(my_y + i, ny), my_y).wait_send()
    sum_ref[core] = gath[core]
    remote(gath.at[1 - core], gath.at[1 - core], ag_s.at[0], ag_r.at[0], other).wait_recv()
    sum_ref[1 - core] = gath[1 - core]
    ag_copy.wait_send()


def finish(qg_ref, sum_ref, qo_ref, wig_ref, wog_ref):
    half, width = sum_ref.shape[1], wog_ref.shape[1]
    qo_ref[...] = qg_ref[...]
    block = jnp.concatenate([sum_ref[0].astype(F32), sum_ref[1].astype(F32)], 0)
    wog_ref[...] = block[:, 0:width]
    wig_ref[...] = block[:, width:].T


def local(n, ngrp, queries, positive, item_feats, frequency, samples, counts, w_in, w_out):
    nx = max(1, math.isqrt(n // 2))
    nz = n // nx
    ny = ngrp // 2
    slots = samples.shape[2]
    items, feat = item_feats.shape
    nq, width = queries.shape
    cb = w_out.shape[0] // n
    lanes = width + feat
    dma = lambda *k: pltpu.SemaphoreType.DMA(k)
    vm = lambda *s: pltpu.VMEM(s, BF16)
    vf = lambda *s: pltpu.VMEM(s, F32)
    vspec = pl.BlockSpec(memory_space=pltpu.VMEM)
    query_grad, sums = pl.pallas_call(
        functools.partial(kernel, (n, ngrp, nx, nz, ny)),
        out_shape=(
            jax.ShapeDtypeStruct((nq, width), F32),
            jax.ShapeDtypeStruct((2, cb // 2, lanes), BF16),
        ),
        in_specs=[vspec] * 5 + [pl.BlockSpec(memory_space=pltpu.SMEM)] + [vspec] * 2,
        out_specs=(vspec,) * 2,
        scratch_shapes=[
            pltpu.VMEM((n, 1, slots), jnp.int32),
            vm(n, items, feat), vm(n, items + 16, width), vm(n, items, width),
            vm(n, slots, width), vm(n, nq, slots), vf(n, nq, slots), vf(nq, slots),
            vm(n, slots, width), vm(n, slots, width),
            vm(n, cb, items), vm(cb, feat), vf(items, width), vf(nq, width),
            vf(cb, width), vf(cb, feat),
            vm(2, cb // 2, lanes), vm(cb // 2, lanes), vm(ny, cb // 2, lanes), vm(2, cb // 2, lanes),
            dma(n), dma(n), dma(n), dma(n), dma(1), dma(1), dma(ny), dma(ny), dma(1), dma(1),
        ]
        + [dma(2, n), dma(2, n), dma(2, n), dma(2, nx, n)] * 3,
        compiler_params=pltpu.CompilerParams(
            collective_id=0, has_side_effects=True, vmem_limit_bytes=56 * 1024 * 1024
        ),
    )(
        queries,
        positive.reshape(1, nq),
        item_feats,
        frequency.reshape(1, items),
        samples.reshape(n, 1, slots),
        counts,
        w_in,
        w_out,
    )
    return pl.pallas_call(
        finish,
        out_shape=(
            jax.ShapeDtypeStruct((nq, width), F32),
            jax.ShapeDtypeStruct((feat, cb), F32),
            jax.ShapeDtypeStruct((cb, width), F32),
        ),
        in_specs=[vspec] * 2,
        out_specs=(vspec,) * 3,
    )(query_grad, sums)


def solution(mesh):
    in_specs = (
        P(("grp", "shard"), None),
        P(("grp", "shard")),
        P(("grp", "shard"), None),
        P(("grp", "shard")),
        P(("grp", "shard"), None, None),
        P(("grp", "shard"), None),
        P(),
        P(),
    )
    out_specs = (P(("grp", "shard"), None), P(None, "shard"), P("shard", None))
    body = functools.partial(local, mesh.shape["shard"], mesh.shape["grp"])
    return jax.shard_map(body, mesh=mesh, in_specs=in_specs, out_specs=out_specs, check_vma=False)
```

```python
import functools
import math

import jax
import jax.numpy as jnp
from jax import lax
from jax.experimental import pallas as pl
from jax.experimental.pallas import tpu as pltpu
from jax.sharding import PartitionSpec as P

inv_temperature = 1.0 / 0.05
log_base = 4.0
epsilon = 1e-06
masked_logit = -10000.0
MESH = pl.DeviceIdType.MESH
F32 = jnp.float32
BF16 = jnp.bfloat16


def mm(left, right, dims):
    return lax.dot_general(left, right, (dims, ((), ())), preferred_element_type=F32)


NN = ((1,), (0,))
NT = ((1,), (1,))
TN = ((0,), (0,))


def kernel(
    dims,
    q_ref, pos_ref, feats_ref, freq_ref, samp_ref, counts_ref, w_in_ref, w_out_ref,
    qg_ref, sum_ref,
    req, fall, uall, rall, neg, ngrad, esc, tot, rsend, rrecv, hidt, wt, acc, uq,
    woacc, wiacc, part, crecv, yall, gath,
    req_s, req_r, bwd_s, bwd_r, core_s, core_r, y_s, y_r, ag_s, ag_r, *ag_sems,
):
    n, ngrp, nx, nz, ny = dims
    few = n <= 8
    width = w_out_ref.shape[1]
    items = feats_ref.shape[0]
    slots = samp_ref.shape[2]
    cb = w_out_ref.shape[0] // n
    g = lax.axis_index("grp")
    me = lax.axis_index("shard")
    core, my_y = lax.rem(g, 2), lax.div(g, 2)
    my_x, my_z = lax.rem(me, nx), lax.div(me, nx)

    def shard_dev(p):
        return {"shard": p}

    def grp_dev(p):
        return {"grp": p}

    def remote(src, dst, ssem, rsem, dev):
        return pltpu.make_async_remote_copy(
            src_ref=src, dst_ref=dst, send_sem=ssem, recv_sem=rsem,
            device_id=dev, device_id_type=MESH,
        )

    class Gather:
        def __init__(self, buf, split, sems):
            self.buf, self.sems, self.sent = buf, sems, []
            self.parts = (pl.ds(0, split), pl.ds(split, buf.shape[1] - split))

        def copy(self, h, block, ssem, dev):
            ref = self.buf.at[block, self.parts[h]]
            return remote(ref, ref, ssem, self.sems[0].at[h, block], dev)

        def send(self, cond, h, block, kind, dev, x=0):
            ssem = self.sems[kind].at[(h, x, block) if kind == 3 else (h, block)]
            make = lambda: self.copy(h, block, ssem, dev)
            pl.when(cond)(lambda: make().start())
            self.sent.append((cond, make))

        def right(self, cond, h, block):
            self.send(cond & (my_z + 1 < nz), h, block, 1, shard_dev(lax.min(me + nx, n - 1)))

        def left(self, cond, h, block):
            self.send(cond & (my_z >= 1), h, block, 2, shard_dev(lax.max(me - nx, 0)))

        def across(self, cond, h, block):
            for i in range(1, nx):
                x = lax.rem(my_x + i, nx)
                self.send(cond, h, block, 3, shard_dev(my_z * nx + x), x)

        def wait(self, cond, h, block):
            pl.when(cond)(
                lambda: self.copy(h, block, self.sems[1].at[h, block], shard_dev(me)).wait_recv()
            )

        def start(self):
            yes = my_z >= 0
            self.right(yes, 0, me)
            self.left(yes, 0, me)
            self.across(yes, 1, me)
            self.across(yes, 0, me)
            self.right(yes, 1, me)
            self.left(yes, 1, me)

        def step(self, k):
            yes = my_z >= 0
            lo, hi = my_z - k >= 0, my_z + k < nz
            zl, zh = lax.max(my_z - k, 0), lax.min(my_z + k, nz - 1)
            if k == 1:
                for i in range(1, nx):
                    block = my_z * nx + lax.rem(my_x + i, nx)
                    self.wait(yes, 1, block)
                    self.right(yes, 1, block)
                    self.left(yes, 1, block)
            for cond, z, onward in ((lo, zl, self.right), (hi, zh, self.left)):
                block = z * nx + my_x
                self.wait(cond, 0, block)
                onward(cond, 0, block)
                self.across(cond, 0, block)
            for i in range(nx):
                for cond, z, onward in ((lo, zl, self.right), (hi, zh, self.left)):
                    block = z * nx + lax.rem(my_x + i, nx)
                    self.wait(cond, 1, block)
                    onward(cond, 1, block)

        def finish(self, z):
            for i in range(1, nx):
                self.wait(my_z >= 0, 0, z * nx + lax.rem(my_x + i, nx))

        def drain(self):
            for cond, make in self.sent:
                pl.when(cond)(lambda: make().wait_send())

        def run(self, work):
            for k in range(1, nz):
                self.step(k)
                for cond, z in (
                    (my_z - k >= 0, lax.max(my_z - k, 0)),
                    (my_z + k < nz, lax.min(my_z + k, nz - 1)),
                ):
                    pl.when(cond)(lambda: work(z * nx + my_x))
            for i in range(1, nx):
                x = lax.rem(my_x + i, nx)

                @pl.loop(0, nz)
                def _(k):
                    z = lax.rem(my_z + k, nz)
                    self.wait(my_z >= 0, 0, z * nx + x)
                    work(z * nx + x)

    barrier = pltpu.get_barrier_semaphore()
    for i in range(1, n):
        pl.semaphore_signal(
            barrier, inc=1, device_id=shard_dev(lax.rem(me + i, n)), device_id_type=MESH
        )
    for i in range(1, ngrp):
        pl.semaphore_signal(
            barrier, inc=1, device_id=grp_dev(lax.rem(g + i, ngrp)), device_id_type=MESH
        )
    fall[me] = feats_ref[...]
    pl.semaphore_wait(barrier, n - 1 + ngrp - 1)

    def req_copy(p, src):
        return remote(samp_ref.at[p], req.at[src], req_s.at[p], req_r.at[src], shard_dev(p))

    def bwd_copy(p, src):
        return remote(rsend.at[p], rrecv.at[src], bwd_s.at[p], bwd_r.at[src], shard_dev(p))

    def to(i):
        return lax.rem(me + i, n)

    def frm(i):
        return lax.rem(me + n - i, n)

    ag_f = Gather(fall, items // 4 * 3, ag_sems[0:4])
    ag_u = Gather(uall, items // 4 * 3 + 16, ag_sems[4:8])
    ag_r_ = Gather(rall, items // 4 * 3, ag_sems[8:12])

    ag_f.start()

    @pl.loop(1, n)
    def _(i):
        req_copy(to(i), me).start()

    req[pl.ds(me, 1)] = samp_ref[pl.ds(me, 1)]

    acc[...] = jnp.zeros_like(acc)
    for k in range(nz):
        if k == nz // 2:
            ag_f.step(1)

        @pl.loop(k * nx, (k + 1) * nx, unroll=True)
        def _(b):
            cols = pl.ds(pl.multiple_of(b * cb, 128), cb)
            pre = mm(feats_ref[...], w_in_ref[:, cols], NN)
            h = jnp.maximum(pre, 0.0).astype(BF16)
            acc[...] += mm(h, w_out_ref[cols, :], NN)

    raw_emb = acc[...]
    radius = jnp.sqrt(jnp.sum(raw_emb * raw_emb, -1, keepdims=True) + epsilon)
    unit = raw_emb / radius
    unit_bf = unit.astype(BF16)
    bias = (log_base - jnp.log(freq_ref[...].astype(F32) + 1.0)).astype(BF16)
    uall[me, 0:items, :] = unit_bf
    uall[me, items:, :] = jnp.broadcast_to(bias.astype(F32), (16, items)).astype(BF16)
    if nz > 2:
        ag_f.step(2)
    ag_u.start()

    queries = q_ref[...].astype(F32)
    query_norm = jnp.sqrt(jnp.sum(queries * queries, -1, keepdims=True) + epsilon)
    query_unit = queries / query_norm
    query_bf = query_unit.astype(BF16)
    pos_pick = (
        lax.broadcasted_iota(jnp.int32, (items, q_ref.shape[0]), 0) == pos_ref[...]
    ).astype(F32).astype(BF16)
    pos_rows = mm(pos_pick, unit_bf, TN)
    pos_logit = jnp.sum(query_bf.astype(F32) * pos_rows, -1, keepdims=True) * inv_temperature
    pos_exp = jnp.exp(pos_logit)

    for k in range(3, nz):
        ag_f.step(k)

    item_iota = lax.broadcasted_iota(jnp.int32, (items, slots), 0)
    slot_iota = lax.broadcasted_iota(jnp.int32, (1, slots), 1)

    def onehot(row):
        return (item_iota == row).astype(F32).astype(BF16)

    tot[...] = jnp.zeros_like(tot)

    def logits(src):
        pick = onehot(samp_ref[src])
        rows = mm(pick, uall[src, 0:items, :], TN).astype(BF16)
        neg[src] = rows
        off = mm(uall[src, items:, :], pick, NN)[0:1]
        off = jnp.where(slot_iota < counts_ref[0, src], off, masked_logit)
        e = jnp.exp(mm(query_bf, rows, NT) * inv_temperature + off)
        esc[src] = e
        tot[...] += e

    logits(me)
    ag_u.run(logits)

    total = pos_exp + jnp.sum(tot[...], -1, keepdims=True)
    scale = inv_temperature / total
    pos_grad = (pos_exp / total - 1.0) * inv_temperature

    def row_grads(src):
        d = (esc[src] * scale).astype(BF16)
        ngrad[src] = d
        return mm(d, query_bf, TN).astype(BF16)

    @pl.loop(1, n, unroll=few)
    def _(i):
        p = to(i)
        rsend[p] = row_grads(p)
        bwd_copy(p, me).start()

    rrecv[me] = row_grads(me)

    uq[...] = pos_grad * pos_rows

    @pl.loop(0, n, unroll=few)
    def _(b):
        uq[...] += mm(ngrad[b], neg[b], NN)

    unit_qgrad = uq[...]
    qg_ref[...] = (
        unit_qgrad - query_unit * jnp.sum(query_unit * unit_qgrad, -1, keepdims=True)
    ) / query_norm

    for z in range(nz):
        ag_f.finish(z)
    wt[...] = w_in_ref[:, pl.ds(pl.multiple_of(me * cb, 128), cb)].astype(F32).T.astype(BF16)

    @pl.loop(0, n, unroll=few)
    def _(b):
        hidt[b] = jnp.maximum(mm(wt[...], fall[b], NT), 0.0).astype(BF16)

    pos_term = pos_grad * query_bf.astype(F32)
    high = pos_term.astype(BF16)
    low = (pos_term - high.astype(F32)).astype(BF16)
    acc[...] = mm(pos_pick, high, NN) + mm(pos_pick, low, NN)
    acc[...] += mm(onehot(req[me]), rrecv[me], NN)

    @pl.loop(1, n)
    def _(i):
        src = frm(i)
        req_copy(src, src).wait_recv()
        pick = onehot(req[src])
        bwd_copy(src, src).wait_recv()
        acc[...] += mm(pick, rrecv[src], NN)

    item_grad = acc[...]
    rall[me] = (
        (item_grad - unit * jnp.sum(unit * item_grad, -1, keepdims=True)) / radius
    ).astype(BF16)
    ag_r_.start()

    woacc[...] = jnp.zeros_like(woacc)
    wiacc[...] = jnp.zeros_like(wiacc)
    block_rows = pl.ds(pl.multiple_of(me * cb, cb), cb)

    def weights(src):
        raw = rall[src]
        ht = hidt[src]
        hg = mm(w_out_ref[block_rows, :], raw, NT)
        pg = jnp.where(ht.astype(F32) > 0.0, hg, 0.0).astype(BF16)
        woacc[...] += mm(ht, raw, NN)
        wiacc[...] += mm(pg, fall[src], NN)

    weights(me)
    ag_r_.run(weights)

    half = cb // 2
    for c in range(2):
        part[c, :, 0:width] = woacc[c * half : (c + 1) * half].astype(BF16)
        part[c, :, width:] = wiacc[c * half : (c + 1) * half].astype(BF16)
    other = grp_dev(g + 1 - 2 * core)
    core_copy = remote(part.at[1 - core], crecv, core_s.at[0], core_r.at[0], other)
    core_copy.start()
    core_copy.wait_recv()
    yall[my_y] = (part[core].astype(F32) + crecv[...].astype(F32)).astype(BF16)

    def y_copy(p, slot):
        return remote(yall.at[my_y], yall.at[slot], y_s.at[p], y_r.at[slot], grp_dev(p * 2 + core))

    for i in range(1, ny):
        y_copy(lax.rem(my_y + i, ny), my_y).start()

    @pl.loop(1, n)
    def _(i):
        p = to(i)
        req_copy(p, me).wait_send()
        bwd_copy(p, me).wait_send()

    core_copy.wait_send()
    for ag in (ag_f, ag_u, ag_r_):
        ag.drain()

    for i in range(1, ny):
        p = lax.rem(my_y + i, ny)
        y_copy(p, p).wait_recv()
    value = yall[0].astype(F32)
    for y in range(1, ny):
        value += yall[y].astype(F32)
    gath[core] = value.astype(BF16)
    ag_copy = remote(gath.at[core], gath.at[core], ag_s.at[0], ag_r.at[0], other)
    ag_copy.start()
    for i in range(1, ny):
        y_copy(lax.rem(my_y + i, ny), my_y).wait_send()
    sum_ref[core] = gath[core]
    remote(gath.at[1 - core], gath.at[1 - core], ag_s.at[0], ag_r.at[0], other).wait_recv()
    sum_ref[1 - core] = gath[1 - core]
    ag_copy.wait_send()


def finish(qg_ref, sum_ref, qo_ref, wig_ref, wog_ref):
    half, width = sum_ref.shape[1], wog_ref.shape[1]
    qo_ref[...] = qg_ref[...]
    block = jnp.concatenate([sum_ref[0].astype(F32), sum_ref[1].astype(F32)], 0)
    wog_ref[...] = block[:, 0:width]
    wig_ref[...] = block[:, width:].T


def local(n, ngrp, queries, positive, item_feats, frequency, samples, counts, w_in, w_out):
    nx = max(1, math.isqrt(n // 2))
    nz = n // nx
    ny = ngrp // 2
    slots = samples.shape[2]
    items, feat = item_feats.shape
    nq, width = queries.shape
    cb = w_out.shape[0] // n
    lanes = width + feat
    dma = lambda *k: pltpu.SemaphoreType.DMA(k)
    vm = lambda *s: pltpu.VMEM(s, BF16)
    vf = lambda *s: pltpu.VMEM(s, F32)
    vspec = pl.BlockSpec(memory_space=pltpu.VMEM)
    query_grad, sums = pl.pallas_call(
        functools.partial(kernel, (n, ngrp, nx, nz, ny)),
        out_shape=(
            jax.ShapeDtypeStruct((nq, width), F32),
            jax.ShapeDtypeStruct((2, cb // 2, lanes), BF16),
        ),
        in_specs=[vspec] * 5 + [pl.BlockSpec(memory_space=pltpu.SMEM)] + [vspec] * 2,
        out_specs=(vspec,) * 2,
        scratch_shapes=[
            pltpu.VMEM((n, 1, slots), jnp.int32),
            vm(n, items, feat), vm(n, items + 16, width), vm(n, items, width),
            vm(n, slots, width), vm(n, nq, slots), vf(n, nq, slots), vf(nq, slots),
            vm(n, slots, width), vm(n, slots, width),
            vm(n, cb, items), vm(cb, feat), vf(items, width), vf(nq, width),
            vf(cb, width), vf(cb, feat),
            vm(2, cb // 2, lanes), vm(cb // 2, lanes), vm(ny, cb // 2, lanes), vm(2, cb // 2, lanes),
            dma(n), dma(n), dma(n), dma(n), dma(1), dma(1), dma(ny), dma(ny), dma(1), dma(1),
        ]
        + [dma(2, n), dma(2, n), dma(2, n), dma(2, nx, n)] * 3,
        compiler_params=pltpu.CompilerParams(
            collective_id=0, has_side_effects=True, vmem_limit_bytes=56 * 1024 * 1024
        ),
    )(
        queries,
        positive.reshape(1, nq),
        item_feats,
        frequency.reshape(1, items),
        samples.reshape(n, 1, slots),
        counts,
        w_in,
        w_out,
    )
    return pl.pallas_call(
        finish,
        out_shape=(
            jax.ShapeDtypeStruct((nq, width), F32),
            jax.ShapeDtypeStruct((feat, cb), F32),
            jax.ShapeDtypeStruct((cb, width), F32),
        ),
        in_specs=[vspec] * 2,
        out_specs=(vspec,) * 3,
    )(query_grad, sums)


def solution(mesh):
    in_specs = (
        P(("grp", "shard"), None),
        P(("grp", "shard")),
        P(("grp", "shard"), None),
        P(("grp", "shard")),
        P(("grp", "shard"), None, None),
        P(("grp", "shard"), None),
        P(),
        P(),
    )
    out_specs = (P(("grp", "shard"), None), P(None, "shard"), P("shard", None))
    body = functools.partial(local, mesh.shape["shard"], mesh.shape["grp"])
    return jax.shard_map(body, mesh=mesh, in_specs=in_specs, out_specs=out_specs, check_vma=False)
```

```python
import functools
import math

import jax
import jax.numpy as jnp
from jax import lax
from jax.experimental import pallas as pl
from jax.experimental.pallas import tpu as pltpu
from jax.sharding import PartitionSpec as P

inv_temperature = 1.0 / 0.05
log_base = 4.0
epsilon = 1e-06
masked_logit = -10000.0
MESH = pl.DeviceIdType.MESH
F32 = jnp.float32
BF16 = jnp.bfloat16


def mm(left, right, dims):
    return lax.dot_general(left, right, (dims, ((), ())), preferred_element_type=F32)


NN = ((1,), (0,))
NT = ((1,), (1,))
TN = ((0,), (0,))


def kernel(
    dims,
    q_ref, pos_ref, feats_ref, freq_ref, samp_ref, counts_ref, w_in_ref, w_out_ref,
    qg_ref, sum_ref,
    req, fall, uall, rall, neg, ngrad, esc, tot, rsend, rrecv, hidt, wt, acc, uq,
    woacc, wiacc, part, crecv, yall, gath,
    req_s, req_r, bwd_s, bwd_r, core_s, core_r, y_s, y_r, ag_s, ag_r, *ag_sems,
):
    n, ngrp, nx, nz, ny = dims
    few = n <= 8
    width = w_out_ref.shape[1]
    items = feats_ref.shape[0]
    slots = samp_ref.shape[2]
    cb = w_out_ref.shape[0] // n
    g = lax.axis_index("grp")
    me = lax.axis_index("shard")
    core, my_y = lax.rem(g, 2), lax.div(g, 2)
    my_x, my_z = lax.rem(me, nx), lax.div(me, nx)

    def shard_dev(p):
        return {"shard": p}

    def grp_dev(p):
        return {"grp": p}

    def remote(src, dst, ssem, rsem, dev):
        return pltpu.make_async_remote_copy(
            src_ref=src, dst_ref=dst, send_sem=ssem, recv_sem=rsem,
            device_id=dev, device_id_type=MESH,
        )

    class Gather:
        def __init__(self, buf, split, sems):
            self.buf, self.sems, self.sent = buf, sems, []
            self.parts = (pl.ds(0, split), pl.ds(split, buf.shape[1] - split))

        def copy(self, h, block, ssem, dev):
            ref = self.buf.at[block, self.parts[h]]
            return remote(ref, ref, ssem, self.sems[0].at[h, block], dev)

        def send(self, cond, h, block, kind, dev, x=0):
            ssem = self.sems[kind].at[(h, x, block) if kind == 3 else (h, block)]
            make = lambda: self.copy(h, block, ssem, dev)
            pl.when(cond)(lambda: make().start())
            self.sent.append((cond, make))

        def right(self, cond, h, block):
            self.send(cond & (my_z + 1 < nz), h, block, 1, shard_dev(lax.min(me + nx, n - 1)))

        def left(self, cond, h, block):
            self.send(cond & (my_z >= 1), h, block, 2, shard_dev(lax.max(me - nx, 0)))

        def across(self, cond, h, block):
            for i in range(1, nx):
                x = lax.rem(my_x + i, nx)
                self.send(cond, h, block, 3, shard_dev(my_z * nx + x), x)

        def wait(self, cond, h, block):
            pl.when(cond)(
                lambda: self.copy(h, block, self.sems[1].at[h, block], shard_dev(me)).wait_recv()
            )

        def start(self):
            yes = my_z >= 0
            self.right(yes, 0, me)
            self.left(yes, 0, me)
            self.across(yes, 1, me)
            self.across(yes, 0, me)
            self.right(yes, 1, me)
            self.left(yes, 1, me)

        def step(self, k):
            yes = my_z >= 0
            lo, hi = my_z - k >= 0, my_z + k < nz
            zl, zh = lax.max(my_z - k, 0), lax.min(my_z + k, nz - 1)
            if k == 1:
                for i in range(1, nx):
                    block = my_z * nx + lax.rem(my_x + i, nx)
                    self.wait(yes, 1, block)
                    self.right(yes, 1, block)
                    self.left(yes, 1, block)
            for cond, z, onward in ((lo, zl, self.right), (hi, zh, self.left)):
                block = z * nx + my_x
                self.wait(cond, 0, block)
                onward(cond, 0, block)
                self.across(cond, 0, block)
            for i in range(nx):
                for cond, z, onward in ((lo, zl, self.right), (hi, zh, self.left)):
                    block = z * nx + lax.rem(my_x + i, nx)
                    self.wait(cond, 1, block)
                    onward(cond, 1, block)

        def finish(self, z):
            for i in range(1, nx):
                self.wait(my_z >= 0, 0, z * nx + lax.rem(my_x + i, nx))

        def drain(self):
            for cond, make in self.sent:
                pl.when(cond)(lambda: make().wait_send())

        def run(self, work):
            for k in range(1, nz):
                self.step(k)
                for cond, z in (
                    (my_z - k >= 0, lax.max(my_z - k, 0)),
                    (my_z + k < nz, lax.min(my_z + k, nz - 1)),
                ):
                    pl.when(cond)(lambda: work(z * nx + my_x))
            for i in range(1, nx):
                x = lax.rem(my_x + i, nx)

                @pl.loop(0, nz)
                def _(k):
                    z = lax.rem(my_z + k, nz)
                    self.wait(my_z >= 0, 0, z * nx + x)
                    work(z * nx + x)

    barrier = pltpu.get_barrier_semaphore()
    for i in range(1, n):
        pl.semaphore_signal(
            barrier, inc=1, device_id=shard_dev(lax.rem(me + i, n)), device_id_type=MESH
        )
    for i in range(1, ngrp):
        pl.semaphore_signal(
            barrier, inc=1, device_id=grp_dev(lax.rem(g + i, ngrp)), device_id_type=MESH
        )
    fall[me] = feats_ref[...]
    pl.semaphore_wait(barrier, n - 1 + ngrp - 1)

    def req_copy(p, src):
        return remote(samp_ref.at[p], req.at[src], req_s.at[p], req_r.at[src], shard_dev(p))

    def bwd_copy(p, src):
        return remote(rsend.at[p], rrecv.at[src], bwd_s.at[p], bwd_r.at[src], shard_dev(p))

    def to(i):
        return lax.rem(me + i, n)

    def frm(i):
        return lax.rem(me + n - i, n)

    ag_f = Gather(fall, items // 2, ag_sems[0:4])
    ag_u = Gather(uall, items // 2 + 16, ag_sems[4:8])
    ag_r_ = Gather(rall, items // 2, ag_sems[8:12])

    ag_f.start()

    @pl.loop(1, n)
    def _(i):
        req_copy(to(i), me).start()

    req[pl.ds(me, 1)] = samp_ref[pl.ds(me, 1)]

    acc[...] = jnp.zeros_like(acc)
    for k in range(nz):
        if k == nz // 2:
            ag_f.step(1)

        @pl.loop(k * nx, (k + 1) * nx, unroll=True)
        def _(b):
            cols = pl.ds(pl.multiple_of(b * cb, 128), cb)
            pre = mm(feats_ref[...], w_in_ref[:, cols], NN)
            h = jnp.maximum(pre, 0.0).astype(BF16)
            acc[...] += mm(h, w_out_ref[cols, :], NN)

    raw_emb = acc[...]
    radius = jnp.sqrt(jnp.sum(raw_emb * raw_emb, -1, keepdims=True) + epsilon)
    unit = raw_emb / radius
    unit_bf = unit.astype(BF16)
    bias = (log_base - jnp.log(freq_ref[...].astype(F32) + 1.0)).astype(BF16)
    uall[me, 0:items, :] = unit_bf
    uall[me, items:, :] = jnp.broadcast_to(bias.astype(F32), (16, items)).astype(BF16)
    if nz > 2:
        ag_f.step(2)
    ag_u.start()

    queries = q_ref[...].astype(F32)
    query_norm = jnp.sqrt(jnp.sum(queries * queries, -1, keepdims=True) + epsilon)
    query_unit = queries / query_norm
    query_bf = query_unit.astype(BF16)
    pos_pick = (
        lax.broadcasted_iota(jnp.int32, (items, q_ref.shape[0]), 0) == pos_ref[...]
    ).astype(F32).astype(BF16)
    pos_rows = mm(pos_pick, unit_bf, TN)
    pos_logit = jnp.sum(query_bf.astype(F32) * pos_rows, -1, keepdims=True) * inv_temperature
    pos_exp = jnp.exp(pos_logit)

    for k in range(3, nz):
        ag_f.step(k)

    item_iota = lax.broadcasted_iota(jnp.int32, (items, slots), 0)
    slot_iota = lax.broadcasted_iota(jnp.int32, (1, slots), 1)

    def onehot(row):
        return (item_iota == row).astype(F32).astype(BF16)

    tot[...] = jnp.zeros_like(tot)

    def logits(src):
        pick = onehot(samp_ref[src])
        rows = mm(pick, uall[src, 0:items, :], TN).astype(BF16)
        neg[src] = rows
        off = mm(uall[src, items:, :], pick, NN)[0:1]
        off = jnp.where(slot_iota < counts_ref[0, src], off, masked_logit)
        e = jnp.exp(mm(query_bf, rows, NT) * inv_temperature + off)
        esc[src] = e
        tot[...] += e

    logits(me)
    ag_u.run(logits)

    total = pos_exp + jnp.sum(tot[...], -1, keepdims=True)
    scale = inv_temperature / total
    pos_grad = (pos_exp / total - 1.0) * inv_temperature

    def row_grads(src):
        d = (esc[src] * scale).astype(BF16)
        ngrad[src] = d
        return mm(d, query_bf, TN).astype(BF16)

    @pl.loop(1, n, unroll=few)
    def _(i):
        p = to(i)
        rsend[p] = row_grads(p)
        bwd_copy(p, me).start()

    rrecv[me] = row_grads(me)

    uq[...] = pos_grad * pos_rows

    @pl.loop(0, n, unroll=few)
    def _(b):
        uq[...] += mm(ngrad[b], neg[b], NN)

    unit_qgrad = uq[...]
    qg_ref[...] = (
        unit_qgrad - query_unit * jnp.sum(query_unit * unit_qgrad, -1, keepdims=True)
    ) / query_norm

    for z in range(nz):
        ag_f.finish(z)
    wt[...] = w_in_ref[:, pl.ds(pl.multiple_of(me * cb, 128), cb)].astype(F32).T.astype(BF16)

    @pl.loop(0, n, unroll=few)
    def _(b):
        hidt[b] = jnp.maximum(mm(wt[...], fall[b], NT), 0.0).astype(BF16)

    pos_term = pos_grad * query_bf.astype(F32)
    high = pos_term.astype(BF16)
    low = (pos_term - high.astype(F32)).astype(BF16)
    acc[...] = mm(pos_pick, high, NN) + mm(pos_pick, low, NN)
    acc[...] += mm(onehot(req[me]), rrecv[me], NN)

    @pl.loop(1, n)
    def _(i):
        src = frm(i)
        req_copy(src, src).wait_recv()
        pick = onehot(req[src])
        bwd_copy(src, src).wait_recv()
        acc[...] += mm(pick, rrecv[src], NN)

    item_grad = acc[...]
    rall[me] = (
        (item_grad - unit * jnp.sum(unit * item_grad, -1, keepdims=True)) / radius
    ).astype(BF16)
    ag_r_.start()

    woacc[...] = jnp.zeros_like(woacc)
    wiacc[...] = jnp.zeros_like(wiacc)
    block_rows = pl.ds(pl.multiple_of(me * cb, cb), cb)

    def weights(src):
        raw = rall[src]
        ht = hidt[src]
        hg = mm(w_out_ref[block_rows, :], raw, NT)
        pg = jnp.where(ht.astype(F32) > 0.0, hg, 0.0).astype(BF16)
        woacc[...] += mm(ht, raw, NN)
        wiacc[...] += mm(pg, fall[src], NN)

    weights(me)
    ag_r_.run(weights)

    half = cb // 2
    for c in range(2):
        part[c, :, 0:width] = woacc[c * half : (c + 1) * half].astype(BF16)
        part[c, :, width:] = wiacc[c * half : (c + 1) * half].astype(BF16)
    other = grp_dev(g + 1 - 2 * core)
    core_copy = remote(part.at[1 - core], crecv, core_s.at[0], core_r.at[0], other)
    core_copy.start()
    core_copy.wait_recv()
    yall[my_y] = (part[core].astype(F32) + crecv[...].astype(F32)).astype(BF16)

    def y_copy(p, slot):
        return remote(yall.at[my_y], yall.at[slot], y_s.at[p], y_r.at[slot], grp_dev(p * 2 + core))

    for i in range(1, ny):
        y_copy(lax.rem(my_y + i, ny), my_y).start()

    @pl.loop(1, n)
    def _(i):
        p = to(i)
        req_copy(p, me).wait_send()
        bwd_copy(p, me).wait_send()

    core_copy.wait_send()
    for ag in (ag_f, ag_u, ag_r_):
        ag.drain()

    for i in range(1, ny):
        p = lax.rem(my_y + i, ny)
        y_copy(p, p).wait_recv()
    value = yall[0].astype(F32)
    for y in range(1, ny):
        value += yall[y].astype(F32)
    gath[core] = value.astype(BF16)
    ag_copy = remote(gath.at[core], gath.at[core], ag_s.at[0], ag_r.at[0], other)
    ag_copy.start()
    for i in range(1, ny):
        y_copy(lax.rem(my_y + i, ny), my_y).wait_send()
    sum_ref[core] = gath[core]
    remote(gath.at[1 - core], gath.at[1 - core], ag_s.at[0], ag_r.at[0], other).wait_recv()
    sum_ref[1 - core] = gath[1 - core]
    ag_copy.wait_send()


def finish(qg_ref, sum_ref, qo_ref, wig_ref, wog_ref):
    half, width = sum_ref.shape[1], wog_ref.shape[1]
    qo_ref[...] = qg_ref[...]
    block = jnp.concatenate([sum_ref[0].astype(F32), sum_ref[1].astype(F32)], 0)
    wog_ref[...] = block[:, 0:width]
    wig_ref[...] = block[:, width:].T


def local(n, ngrp, queries, positive, item_feats, frequency, samples, counts, w_in, w_out):
    nx = max(1, math.isqrt(n // 2))
    nz = n // nx
    ny = ngrp // 2
    slots = samples.shape[2]
    items, feat = item_feats.shape
    nq, width = queries.shape
    cb = w_out.shape[0] // n
    lanes = width + feat
    dma = lambda *k: pltpu.SemaphoreType.DMA(k)
    vm = lambda *s: pltpu.VMEM(s, BF16)
    vf = lambda *s: pltpu.VMEM(s, F32)
    vspec = pl.BlockSpec(memory_space=pltpu.VMEM)
    query_grad, sums = pl.pallas_call(
        functools.partial(kernel, (n, ngrp, nx, nz, ny)),
        out_shape=(
            jax.ShapeDtypeStruct((nq, width), F32),
            jax.ShapeDtypeStruct((2, cb // 2, lanes), BF16),
        ),
        in_specs=[vspec] * 5 + [pl.BlockSpec(memory_space=pltpu.SMEM)] + [vspec] * 2,
        out_specs=(vspec,) * 2,
        scratch_shapes=[
            pltpu.VMEM((n, 1, slots), jnp.int32),
            vm(n, items, feat), vm(n, items + 16, width), vm(n, items, width),
            vm(n, slots, width), vm(n, nq, slots), vf(n, nq, slots), vf(nq, slots),
            vm(n, slots, width), vm(n, slots, width),
            vm(n, cb, items), vm(cb, feat), vf(items, width), vf(nq, width),
            vf(cb, width), vf(cb, feat),
            vm(2, cb // 2, lanes), vm(cb // 2, lanes), vm(ny, cb // 2, lanes), vm(2, cb // 2, lanes),
            dma(n), dma(n), dma(n), dma(n), dma(1), dma(1), dma(ny), dma(ny), dma(1), dma(1),
        ]
        + [dma(2, n), dma(2, n), dma(2, n), dma(2, nx, n)] * 3,
        compiler_params=pltpu.CompilerParams(
            collective_id=0, has_side_effects=True, vmem_limit_bytes=56 * 1024 * 1024
        ),
    )(
        queries,
        positive.reshape(1, nq),
        item_feats,
        frequency.reshape(1, items),
        samples.reshape(n, 1, slots),
        counts,
        w_in,
        w_out,
    )
    return pl.pallas_call(
        finish,
        out_shape=(
            jax.ShapeDtypeStruct((nq, width), F32),
            jax.ShapeDtypeStruct((feat, cb), F32),
            jax.ShapeDtypeStruct((cb, width), F32),
        ),
        in_specs=[vspec] * 2,
        out_specs=(vspec,) * 3,
    )(query_grad, sums)


def solution(mesh):
    in_specs = (
        P(("grp", "shard"), None),
        P(("grp", "shard")),
        P(("grp", "shard"), None),
        P(("grp", "shard")),
        P(("grp", "shard"), None, None),
        P(("grp", "shard"), None),
        P(),
        P(),
    )
    out_specs = (P(("grp", "shard"), None), P(None, "shard"), P("shard", None))
    body = functools.partial(local, mesh.shape["shard"], mesh.shape["grp"])
    return jax.shard_map(body, mesh=mesh, in_specs=in_specs, out_specs=out_specs, check_vma=False)
```
